32 devices in a mesh: gx: 2 (over y), gy: 4 (over z), gz: 4 (over x, core).
Axes of the slice: x: 2, y: 2, z: 4, core: 2. Of those that a mesh axis runs over, the one named last changes fastest.
Arguments:
- load_cases: float32 [2, 128, 32, 256], P(None, 'gz', 'gy', 'gx'), may hold values from -6 to 6
- density_level: int32 [128, 32, 256], P('gz', 'gy', 'gx'), may hold values from 0 to 7
Outputs:
- solution: float32 [2, 128, 32, 256], P(None, 'gz', 'gy', 'gx')
The draws below stay inside these ranges and needn't reach their ends.
All inputs are finite; a program needn't handle non-finite values.
Results may differ from the reference program's by a relative error of at most 0.00011.
Values sent between devices are 32-bit elements; how exact they have to be, the bound alone decides.
A program may use at most 192 MiB of HBM per device.

```python
import math
import jax
import jax.numpy as jnp

CASES = 2
LEVELS = 8
NX = 256
NY = 32
NZ = 128


def draw_load_cases(key, part):
    full_shape = (CASES, NZ, NY, NX)
    return jnp.clip(jax.random.normal(key, full_shape, jnp.float32), -6.0, 6.0)


def plant(result, key, least, high):
    place = [jax.random.randint(jax.random.fold_in(key, axis), (), 0, length) for axis, length in enumerate(result.shape)]
    longest = result.shape.index(max(result.shape))
    neighbour = place[:longest] + [(place[longest] + 1) % result.shape[longest]] + place[longest + 1:]
    return result.at[tuple(place)].set(least).at[tuple(neighbour)].set(high)


def setup_inputs(seed: int = 0) -> dict:
    key_list = jax.random.split(jax.random.key(seed), 3)
    return {
        "load_cases": draw_load_cases(jax.random.fold_in(key_list[2], 71), 0),
        "density_level": plant(jax.random.randint(key_list[1], (NZ, NY, NX), 0, LEVELS), jax.random.fold_in(key_list[1], 1), 0, LEVELS - 1).astype(jnp.int32),
    }


middle_point = 0.646875
half_range = 0.503125
first_weight = 1.0 / (middle_point + half_range * math.cos(math.pi / 4))
second_weight = 1.0 / (middle_point - half_range * math.cos(math.pi / 4))


def smooth_sum(padded):
    padded = 0.5 * padded[:, :-2] + padded[:, 1:-1] + 0.5 * padded[:, 2:]
    padded = 0.5 * padded[:, :, :-2] + padded[:, :, 1:-1] + 0.5 * padded[:, :, 2:]
    return 0.5 * padded[..., :-2] + padded[..., 1:-1] + 0.5 * padded[..., 2:]


def operate(values, stiffness, spacing_sq):
    padded = jnp.pad(values, ((0, 0), (1, 1), (1, 1), (1, 1)))
    return stiffness * (16.0 * values - 2.0 * smooth_sum(padded)) / spacing_sq


def jacobi(residue, stiffness, spacing_sq):
    return residue * (spacing_sq / (14.0 * stiffness))


def restrict(values):
    return values.reshape(values.shape[0], values.shape[1] // 2, 2, values.shape[2] // 2, 2, values.shape[3] // 2, 2).mean(axis=(2, 4, 6))


def prolong(values):
    return jnp.repeat(jnp.repeat(jnp.repeat(values, 2, axis=1), 2, axis=2), 2, axis=3)


def presmooth(target, stiffness, spacing_sq):
    guess = first_weight * jacobi(target, stiffness, spacing_sq)
    return guess + second_weight * jacobi(target - operate(guess, stiffness, spacing_sq), stiffness, spacing_sq)


def postsmooth(guess, target, stiffness, spacing_sq):
    guess = guess + first_weight * jacobi(target - operate(guess, stiffness, spacing_sq), stiffness, spacing_sq)
    return guess + second_weight * jacobi(target - operate(guess, stiffness, spacing_sq), stiffness, spacing_sq)


def reference(load_cases, density_level):
    stiffness_fine = (0.05 + 0.95 * (density_level.astype(jnp.float32) / (LEVELS - 1)) ** 3)[None]
    guess_fine = presmooth(load_cases, stiffness_fine, 1.0)
    rhs_mid = restrict(load_cases - operate(guess_fine, stiffness_fine, 1.0))
    stiffness_mid = restrict(stiffness_fine)
    guess_mid = presmooth(rhs_mid, stiffness_mid, 4.0)
    rhs_low = restrict(rhs_mid - operate(guess_mid, stiffness_mid, 4.0))
    stiffness_low = restrict(stiffness_mid)
    guess_low = presmooth(rhs_low, stiffness_low, 16.0)
    rhs_base = restrict(rhs_low - operate(guess_low, stiffness_low, 16.0))
    stiffness_base = restrict(stiffness_low)
    guess_base = postsmooth(presmooth(rhs_base, stiffness_base, 64.0), rhs_base, stiffness_base, 64.0)
    guess_low = postsmooth(guess_low + prolong(guess_base), rhs_low, stiffness_low, 16.0)
    guess_mid = postsmooth(guess_mid + prolong(guess_low), rhs_mid, stiffness_mid, 4.0)
    return postsmooth(guess_fine + prolong(guess_mid), load_cases, stiffness_fine, 1.0)
```

```python
import math

import jax
import jax.numpy as jnp
from jax import lax
from jax.sharding import PartitionSpec as P

LEVELS = 8


middle_point = 0.646875
half_range = 0.503125
first_weight = 1.0 / (middle_point + half_range * math.cos(math.pi / 4))
second_weight = 1.0 / (middle_point - half_range * math.cos(math.pi / 4))


def with_halo(cells, sides, width):
    for axis, dim in sides:
        count = lax.axis_size(axis)
        ends = count - 1
        head = lax.slice_in_dim(cells, 0, width, axis=dim)
        tail = lax.slice_in_dim(cells, cells.shape[dim] - width, cells.shape[dim], axis=dim)
        cells = jnp.concatenate(
            [
                lax.ppermute(tail, axis, [(i, (i + 1) % count) for i in range(ends)]),
                cells,
                lax.ppermute(head, axis, [((i + 1) % count, i) for i in range(ends)]),
            ],
            axis=dim,
        )
    return cells


def smooth_sum(padded):
    padded = 0.5 * padded[:, :-2] + padded[:, 1:-1] + 0.5 * padded[:, 2:]
    padded = 0.5 * padded[:, :, :-2] + padded[:, :, 1:-1] + 0.5 * padded[:, :, 2:]
    return 0.5 * padded[..., :-2] + padded[..., 1:-1] + 0.5 * padded[..., 2:]


def prune(values, have, want):
    cut = have - want
    if cut == 0:
        return values
    return values[
        :, cut : values.shape[1] - cut, cut : values.shape[2] - cut, cut : values.shape[3] - cut
    ]


def inside(own, halo):
    flags = []
    for axis, size in zip(("gz", "gy", "gx"), own):
        start = lax.axis_index(axis) * size
        index = start - halo + lax.iota(jnp.int32, size + 2 * halo)
        flags.append((index >= 0) & (index < size * lax.axis_size(axis)))
    return (
        flags[0][:, None, None] & flags[1][None, :, None] & flags[2][None, None, :]
    ).astype(jnp.float32)


def step(guess, scaled, weight, mask):
    centre = prune(guess, 1, 0)
    applied = (16.0 * centre - 2.0 * smooth_sum(guess)) * (1.0 / 14.0)
    return centre + weight * (scaled - mask * applied)


def restrict(values):
    return values.reshape(
        values.shape[0], values.shape[1] // 2, 2, values.shape[2] // 2, 2, values.shape[3] // 2, 2
    ).mean(axis=(2, 4, 6))


def prolong(values):
    return jnp.repeat(jnp.repeat(jnp.repeat(values, 2, axis=1), 2, axis=2), 2, axis=3)


def framed(values, width=1):
    return jnp.pad(values, ((0, 0), (width, width), (width, width), (width, width)))


def residual(target, stiffness, guess, spacing_sq):
    centre = prune(guess, 1, 0)
    return target - stiffness * (16.0 * centre - 2.0 * smooth_sum(guess)) * (1.0 / spacing_sq)


def coarse_cycle(rhs_low, stiffness_low):
    scaled_low = rhs_low * (16.0 / (14.0 * stiffness_low))
    guess_low = step(framed(first_weight * scaled_low), scaled_low, second_weight, 1.0)
    rhs_base = restrict(residual(rhs_low, stiffness_low, framed(guess_low), 16.0))
    stiffness_base = restrict(stiffness_low)
    scaled_base = rhs_base * (64.0 / (14.0 * stiffness_base))
    guess_base = step(framed(first_weight * scaled_base), scaled_base, second_weight, 1.0)
    guess_base = step(framed(guess_base), scaled_base, first_weight, 1.0)
    guess_base = step(framed(guess_base), scaled_base, second_weight, 1.0)
    guess_low = guess_low + prolong(guess_base)
    guess_low = step(framed(guess_low), scaled_low, first_weight, 1.0)
    return step(framed(guess_low), scaled_low, second_weight, 1.0)


def joined(values):
    for axis, dim in (("gx", 3), ("gy", 2), ("gz", 1)):
        values = lax.all_gather(values, axis, axis=dim, tiled=True)
    return values


SIDES = (("gx", 3), ("gy", 2), ("gz", 1))


def body(load_cases, density_level):
    stiffness_fine = (0.05 + 0.95 * (density_level.astype(jnp.float32) / (LEVELS - 1)) ** 3)[None]
    stiffness_mid = restrict(stiffness_fine)
    stiffness_low = restrict(stiffness_mid)
    own = load_cases.shape[1:]
    own_mid = tuple(size // 2 for size in own)
    own_low = tuple(size // 4 for size in own)
    scaled_fine = with_halo(load_cases * (1.0 / (14.0 * stiffness_fine)), SIDES, 3)
    mask_fine = inside(own, 2)
    guess_fine = step(
        first_weight * scaled_fine, prune(scaled_fine, 3, 2), second_weight, mask_fine
    )
    rhs_mid = restrict(residual(load_cases, stiffness_fine, prune(guess_fine, 2, 1), 1.0))
    scaled_mid = with_halo(rhs_mid * (4.0 / (14.0 * stiffness_mid)), SIDES, 4)
    mask_mid = inside(own_mid, 3)
    guess_mid = step(first_weight * scaled_mid, prune(scaled_mid, 4, 3), second_weight, mask_mid)
    rhs_low = restrict(residual(rhs_mid, stiffness_mid, prune(guess_mid, 3, 1), 4.0))
    guess_low = framed(coarse_cycle(joined(rhs_low), joined(stiffness_low)), 2)
    guess_low = lax.dynamic_slice(
        guess_low,
        (0,) + tuple(lax.axis_index(a) * n for a, n in zip(("gz", "gy", "gx"), own_low)),
        (guess_low.shape[0],) + tuple(n + 4 for n in own_low),
    )
    guess_mid = guess_mid + prune(prolong(guess_low), 4, 3)
    guess_mid = step(guess_mid, prune(scaled_mid, 4, 2), first_weight, prune(mask_mid[None], 3, 2))
    guess_mid = step(guess_mid, prune(scaled_mid, 4, 1), second_weight, prune(mask_mid[None], 3, 1))
    guess_fine = guess_fine + prolong(guess_mid)
    guess_fine = step(
        guess_fine, prune(scaled_fine, 3, 1), first_weight, prune(mask_fine[None], 2, 1)
    )
    return step(guess_fine, prune(scaled_fine, 3, 0), second_weight, 1.0)


def solution(mesh):
    in_specs = (P(None, "gz", "gy", "gx"), P("gz", "gy", "gx"))
    out_specs = P(None, "gz", "gy", "gx")
    return jax.shard_map(body, mesh=mesh, in_specs=in_specs, out_specs=out_specs, check_vma=False)
```

```python
import math

import jax
import jax.numpy as jnp
from jax import lax
from jax.experimental import pallas as pl
from jax.experimental.pallas import tpu as pltpu
from jax.sharding import PartitionSpec as P

LEVELS = 8


middle_point = 0.646875
half_range = 0.503125
first_weight = 1.0 / (middle_point + half_range * math.cos(math.pi / 4))
second_weight = 1.0 / (middle_point - half_range * math.cos(math.pi / 4))


def with_halo(cells, sides, width):
    for axis, dim in sides:
        count = lax.axis_size(axis)
        ends = count - 1
        head = lax.slice_in_dim(cells, 0, width, axis=dim)
        tail = lax.slice_in_dim(cells, cells.shape[dim] - width, cells.shape[dim], axis=dim)
        cells = jnp.concatenate(
            [
                lax.ppermute(tail, axis, [(i, (i + 1) % count) for i in range(ends)]),
                cells,
                lax.ppermute(head, axis, [((i + 1) % count, i) for i in range(ends)]),
            ],
            axis=dim,
        )
    return cells


def smooth_sum(padded):
    padded = 0.5 * padded[:, :-2] + padded[:, 1:-1] + 0.5 * padded[:, 2:]
    padded = 0.5 * padded[:, :, :-2] + padded[:, :, 1:-1] + 0.5 * padded[:, :, 2:]
    return 0.5 * padded[..., :-2] + padded[..., 1:-1] + 0.5 * padded[..., 2:]


def prune(values, have, want):
    cut = have - want
    if cut == 0:
        return values
    return values[
        :, cut : values.shape[1] - cut, cut : values.shape[2] - cut, cut : values.shape[3] - cut
    ]


def inside(own, halo):
    flags = []
    for axis, size in zip(("gz", "gy", "gx"), own):
        start = lax.axis_index(axis) * size
        index = start - halo + lax.iota(jnp.int32, size + 2 * halo)
        flags.append((index >= 0) & (index < size * lax.axis_size(axis)))
    return (
        flags[0][:, None, None] & flags[1][None, :, None] & flags[2][None, None, :]
    ).astype(jnp.float32)


def step(guess, scaled, weight, mask):
    centre = prune(guess, 1, 0)
    applied = (16.0 * centre - 2.0 * smooth_sum(guess)) * (1.0 / 14.0)
    return centre + weight * (scaled - mask * applied)


def restrict(values):
    return values.reshape(
        values.shape[0], values.shape[1] // 2, 2, values.shape[2] // 2, 2, values.shape[3] // 2, 2
    ).mean(axis=(2, 4, 6))


def prolong(values):
    return jnp.repeat(jnp.repeat(jnp.repeat(values, 2, axis=1), 2, axis=2), 2, axis=3)


def framed(values, width=1):
    return jnp.pad(values, ((0, 0), (width, width), (width, width), (width, width)))


def residual(target, stiffness, guess, spacing_sq):
    centre = prune(guess, 1, 0)
    return target - stiffness * (16.0 * centre - 2.0 * smooth_sum(guess)) * (1.0 / spacing_sq)


def coarse_cycle(rhs_low, stiffness_low):
    scaled_low = rhs_low * (16.0 / (14.0 * stiffness_low))
    guess_low = step(framed(first_weight * scaled_low), scaled_low, second_weight, 1.0)
    rhs_base = restrict(residual(rhs_low, stiffness_low, framed(guess_low), 16.0))
    stiffness_base = restrict(stiffness_low)
    scaled_base = rhs_base * (64.0 / (14.0 * stiffness_base))
    guess_base = step(framed(first_weight * scaled_base), scaled_base, second_weight, 1.0)
    guess_base = step(framed(guess_base), scaled_base, first_weight, 1.0)
    guess_base = step(framed(guess_base), scaled_base, second_weight, 1.0)
    guess_low = guess_low + prolong(guess_base)
    guess_low = step(framed(guess_low), scaled_low, first_weight, 1.0)
    return step(framed(guess_low), scaled_low, second_weight, 1.0)


def joined(values):
    for axis, dim in (("gx", 3), ("gy", 2), ("gz", 1)):
        values = lax.all_gather(values, axis, axis=dim, tiled=True)
    return values


SIDES = (("gx", 3), ("gy", 2), ("gz", 1))


def body(load_cases, density_level):
    stiffness_fine = (0.05 + 0.95 * (density_level.astype(jnp.float32) / (LEVELS - 1)) ** 3)[None]
    stiffness_mid = restrict(stiffness_fine)
    stiffness_low = restrict(stiffness_mid)
    own = load_cases.shape[1:]
    own_mid = tuple(size // 2 for size in own)
    own_low = tuple(size // 4 for size in own)
    scaled_fine = with_halo(load_cases * (1.0 / (14.0 * stiffness_fine)), SIDES, 3)
    mask_fine = inside(own, 2)
    guess_fine = step(
        first_weight * scaled_fine, prune(scaled_fine, 3, 2), second_weight, mask_fine
    )
    rhs_mid = restrict(residual(load_cases, stiffness_fine, prune(guess_fine, 2, 1), 1.0))
    scaled_mid = with_halo(rhs_mid * (4.0 / (14.0 * stiffness_mid)), SIDES, 4)
    mask_mid = inside(own_mid, 3)
    guess_mid = step(first_weight * scaled_mid, prune(scaled_mid, 4, 3), second_weight, mask_mid)
    rhs_low = restrict(residual(rhs_mid, stiffness_mid, prune(guess_mid, 3, 1), 4.0))
    guess_low = framed(coarse_cycle(joined(rhs_low), joined(stiffness_low)), 2)
    guess_low = lax.dynamic_slice(
        guess_low,
        (0,) + tuple(lax.axis_index(a) * n for a, n in zip(("gz", "gy", "gx"), own_low)),
        (guess_low.shape[0],) + tuple(n + 4 for n in own_low),
    )
    guess_mid = guess_mid + prune(prolong(guess_low), 4, 3)
    guess_mid = step(guess_mid, prune(scaled_mid, 4, 2), first_weight, prune(mask_mid[None], 3, 2))
    guess_mid = step(guess_mid, prune(scaled_mid, 4, 1), second_weight, prune(mask_mid[None], 3, 1))
    guess_fine = guess_fine + prolong(guess_mid)
    guess_fine = step(
        guess_fine, prune(scaled_fine, 3, 1), first_weight, prune(mask_fine[None], 2, 1)
    )
    return step(guess_fine, prune(scaled_fine, 3, 0), second_weight, 1.0)


HIGHEST = lax.Precision.HIGHEST


def dot(a, b):
    return jnp.dot(a, b, precision=HIGHEST, preferred_element_type=jnp.float32)


def iota(shape, dim):
    return lax.broadcasted_iota(jnp.int32, shape, dim)


def pick(condition):
    return jnp.where(condition, 1.0, 0.0).astype(jnp.float32)


def blur(u, close_z=False):
    rows, depth, length = u.shape
    v = u[1:-1] + 0.5 * (u[:-2] + u[2:])
    down, up = pltpu.roll(v, 1, 1), pltpu.roll(v, depth - 1, 1)
    if close_z:
        z = iota((1, depth, length), 1)
        down, up = down * pick(z > 0), up * pick(z < depth - 1)
    v = v + 0.5 * (down + up)
    x = iota((1, 1, length), 2)
    down, up = pltpu.roll(v, 1, 2) * pick(x > 0), pltpu.roll(v, length - 1, 2) * pick(x < length - 1)
    return v + 0.5 * (down + up)


def move(guess, scaled, weight, mask):
    applied = (16.0 / 14.0) * guess[1:-1] - (2.0 / 14.0) * blur(guess)
    return (guess[1:-1] + weight * (scaled - applied)) * mask


def move_whole(guess, scaled, weight, mask):
    edge = jnp.zeros((1,) + guess.shape[1:], jnp.float32)
    total = blur(jnp.concatenate([edge, guess, edge], 0), True)
    return (guess + weight * (scaled - ((16.0 / 14.0) * guess - (2.0 / 14.0) * total))) * mask


def halve(values, length_out, first=0):
    rows, depth, length = values.shape
    values = values.reshape(rows // 2, 2, depth, length)
    values = values[:, 0] + values[:, 1]
    pairs = (rows // 2) * depth
    across = pick(iota((length, length_out), 0) // 2 + first == iota((length, length_out), 1)) * 0.125
    along = pick(iota((pairs // 2, pairs), 1) // 2 == iota((pairs // 2, pairs), 0))
    flat = dot(along, dot(values.reshape(pairs, length), across))
    return flat.reshape(rows // 2, depth // 2, length_out)


def double(values, depth_out, offset, length_out):
    rows, depth, length = values.shape
    across = pick(iota((length, length_out), 1) // 2 == iota((length, length_out), 0))
    along = pick(iota((depth_out, depth), 0) // 2 + offset == iota((depth_out, depth), 1))
    wide = dot(values.reshape(rows * depth, length), across).reshape(rows, depth, length_out)
    tall = [dot(along, wide[row]) for row in range(rows)]
    return jnp.stack([tall[row // 2] for row in range(2 * rows)], 0)


def domain(rows, depth, length, halo_y, halo_z, own_y, own_z, me_y, me_z, ny, nz):
    y = iota((rows, 1, length), 0) + (me_y * own_y - halo_y)
    z = iota((1, depth, length), 1) + (me_z * own_z - halo_z)
    return pick((y >= 0) & (y < own_y * ny)) * pick((z >= 0) & (z < own_z * nz))


SHIFTS = tuple((dy, dz) for dy in (-1, 0, 1) for dz in (-1, 0, 1))


def kernel(ny, nz, g_ref, b_ref, s_ref, out_ref, gbuf, bbuf, sbuf, mbuf, lbuf, wide, obuf, rbuf,
           send_a, recv_a, send_b, recv_b, send_c, recv_c, send_d, recv_d):
    c, my, mz = lax.axis_index("gx"), lax.axis_index("gy"), lax.axis_index("gz")
    other = 1 - c
    oy, oz, ox = s_ref.shape

    def at(k, y, z):
        return {"gx": k, "gy": y, "gz": z}

    def near(dy, dz):
        return lax.rem(my + dy + ny, ny), lax.rem(mz + dz + nz, nz)

    def group(step):
        index = lax.rem(my * nz + mz + step, ny * nz)
        return index // nz, lax.rem(index, nz)

    barrier = pltpu.get_barrier_semaphore()
    for step in range(1, ny * nz):
        pl.semaphore_signal(barrier, 1, device_id=at(c, *group(step)), device_id_type=pl.DeviceIdType.MESH)
    for shift in SHIFTS:
        pl.semaphore_signal(barrier, 1, device_id=at(other, *near(*shift)), device_id_type=pl.DeviceIdType.MESH)
    gbuf[c, 3 : 3 + oy, 8 : 8 + oz, :] = g_ref[c]
    bbuf[c] = b_ref[c]
    sbuf[c] = s_ref[...]
    pl.semaphore_wait(barrier, ny * nz - 1 + 9)

    def remote(src, dst, sends, recvs, slot, device):
        copy = pltpu.make_async_remote_copy(
            src_ref=src, dst_ref=dst, send_sem=sends.at[slot], recv_sem=recvs.at[slot],
            device_id=device, device_id_type=pl.DeviceIdType.MESH,
        )
        copy.start()
        return copy

    def cut(shift, own, reach, room):
        if shift == 0:
            return 0, room, own
        return (own - reach, room - reach, reach) if shift > 0 else (0, room + own, reach)

    phase = []
    slot = 0
    for k, who in ((0, other), (1, c)):
        for dy, dz in SHIFTS:
            if k == 1 and (dy, dz) == (0, 0):
                continue
            fy, ty, ly = cut(dy, oy, 3, 3)
            fz, tz, lz = cut(dz, oz, 8, 8)
            phase.append(remote(
                g_ref.at[who, fy : fy + ly, fz : fz + lz, :],
                gbuf.at[c, ty : ty + ly, tz : tz + lz, :],
                send_a, recv_a, slot, at(who, *near(dy, dz)),
            ))
            slot += 1
    phase.append(remote(b_ref.at[other], bbuf.at[c], send_a, recv_a, slot, at(other, my, mz)))
    phase.append(remote(s_ref, sbuf.at[c], send_a, recv_a, slot + 1, at(other, my, mz)))
    for copy in phase:
        copy.wait()

    length = 2 * ox
    depth = oz + 16
    fine = (depth, length, )
    def mask_fine(halo):
        return domain(oy + 2 * halo, depth, length, halo, 8, oy, oz, my, mz, ny, nz)
    scaled = jnp.concatenate([gbuf[0], gbuf[1]], -1) * mask_fine(3)
    target = jnp.concatenate([bbuf[0], bbuf[1]], -1)
    stiff = jnp.concatenate([sbuf[0], sbuf[1]], -1)
    guess = move(first_weight * scaled, scaled[1:-1], second_weight, mask_fine(2))
    applied = 16.0 * guess[2:-2] - 2.0 * blur(guess[1:-1])
    rhs_mid = halve(target - stiff * applied[:, 8 : 8 + oz], ox)
    stiff_mid = halve(stiff, ox)

    hy, hz = oy // 2, oz // 2
    mbuf[4 : 4 + hy, 8 : 8 + hz, :] = rhs_mid * (4.0 / (14.0 * stiff_mid))
    phase = []
    for slot, (dy, dz) in enumerate(shift for shift in SHIFTS if shift != (0, 0)):
        fy, ty, ly = cut(dy, hy, 4, 4)
        fz, tz, lz = cut(dz, hz, 8, 8)
        phase.append(remote(
            mbuf.at[4 + fy : 4 + fy + ly, 8 + fz : 8 + fz + lz, :],
            mbuf.at[ty : ty + ly, tz : tz + lz, :],
            send_b, recv_b, slot, at(c, *near(dy, dz)),
        ))
    packed_stiff = halve(stiff_mid, ox, ox // 2)
    for copy in phase:
        copy.wait()

    def mask_mid(halo):
        return domain(hy + 2 * halo, hz + 16, ox, halo, 8, hy, hz, my, mz, ny, nz)
    scaled_mid = mbuf[...] * mask_mid(4)
    guess_mid = move(first_weight * scaled_mid, scaled_mid[1:-1], second_weight, mask_mid(3))
    applied = 16.0 * guess_mid[3:-3] - 2.0 * blur(guess_mid[2:-2])
    residue = rhs_mid - stiff_mid * applied[:, 8 : 8 + hz] * 0.25

    qy, qz = oy // 4, oz // 4
    lbuf[mz, my] = halve(residue, ox) + packed_stiff
    phase = []
    for step in range(1, ny * nz):
        phase.append(remote(
            lbuf.at[mz, my], lbuf.at[mz, my], send_c, recv_c, step - 1, at(c, *group(step))
        ))
    for copy in phase:
        copy.wait()
    packed = jnp.concatenate(
        [jnp.concatenate([lbuf[z, y] for y in range(ny)], 0) for z in range(nz)], 1
    )
    x = iota((1, 1, ox), 2)
    mask_low, mask_base = pick(x < ox // 2), pick(x < ox // 4)
    rhs_low = packed * mask_low
    stiff_low = pltpu.roll(packed, ox // 2, 2) * mask_low + (1.0 - mask_low)
    scaled_low = rhs_low * (16.0 / (14.0 * stiff_low))
    guess_low = move_whole(first_weight * scaled_low, scaled_low, second_weight, mask_low)
    edge = jnp.zeros((1,) + guess_low.shape[1:], jnp.float32)
    applied = 16.0 * guess_low - 2.0 * blur(jnp.concatenate([edge, guess_low, edge], 0), True)
    rhs_base = halve((rhs_low - stiff_low * applied * 0.0625) * mask_low, ox)
    stiff_base = halve(stiff_low, ox) * mask_base + (1.0 - mask_base)
    scaled_base = rhs_base * (64.0 / (14.0 * stiff_base))
    guess_base = move_whole(first_weight * scaled_base, scaled_base, second_weight, mask_base)
    guess_base = move_whole(guess_base, scaled_base, first_weight, mask_base)
    guess_base = move_whole(guess_base, scaled_base, second_weight, mask_base)
    guess_low = guess_low + double(guess_base, qz * nz, 0, ox)
    guess_low = move_whole(guess_low, scaled_low, first_weight, mask_low)
    guess_low = move_whole(guess_low, scaled_low, second_weight, mask_low)

    wide[...] = jnp.zeros(wide.shape, jnp.float32)
    wide[2 : 2 + qy * ny, 8 : 8 + qz * nz, :] = guess_low
    around = wide[pl.ds(my * qy, qy + 4), pl.ds(pl.multiple_of(mz * qz, 8), qz + 16), :]
    guess_mid = guess_mid + double(around, hz + 16, 4, ox)[1:-1]
    guess_mid = move(guess_mid, scaled_mid[2:-2], first_weight, mask_mid(2))
    guess_mid = move(guess_mid, scaled_mid[3:-3], second_weight, mask_mid(1))
    guess = guess + double(guess_mid, depth, 4, length)
    guess = move(guess, scaled[2:-2], first_weight, mask_fine(1))
    guess = move(guess, scaled[3:-3], second_weight, 1.0)[:, 8 : 8 + oz]

    obuf[0] = guess[:, :, :ox]
    obuf[1] = guess[:, :, ox:]
    copy = remote(obuf.at[other], rbuf, send_d, recv_d, 0, at(other, my, mz))
    out_ref[c] = obuf[c]
    copy.wait()
    out_ref[other] = rbuf[...]


def split_cases(ny, nz, load_cases, density_level):
    stiffness = (0.05 + 0.95 * (density_level.astype(jnp.float32) / (LEVELS - 1)) ** 3)
    stiffness = stiffness.transpose(1, 0, 2)
    target = load_cases.transpose(0, 2, 1, 3)
    scaled = target * (1.0 / (14.0 * stiffness))
    oy, oz, ox = stiffness.shape
    f32 = jnp.float32
    spec = pl.BlockSpec(memory_space=pltpu.VMEM)
    dma = pltpu.SemaphoreType.DMA
    many = ny * nz - 1
    out = pl.pallas_call(
        lambda *refs: kernel(ny, nz, *refs),
        out_shape=jax.ShapeDtypeStruct(target.shape, f32),
        in_specs=[spec] * 3,
        out_specs=spec,
        scratch_shapes=[
            pltpu.VMEM((2, oy + 6, oz + 16, ox), f32),
            pltpu.VMEM((2, oy, oz, ox), f32),
            pltpu.VMEM((2, oy, oz, ox), f32),
            pltpu.VMEM((oy // 2 + 8, oz // 2 + 16, ox), f32),
            pltpu.VMEM((nz, ny, oy // 4, oz // 4, ox), f32),
            pltpu.VMEM((oy // 4 * ny + 4, oz // 4 * nz + 16, ox), f32),
            pltpu.VMEM((2, oy, oz, ox), f32),
            pltpu.VMEM((oy, oz, ox), f32),
            dma((19,)), dma((19,)), dma((8,)), dma((8,)), dma((many,)), dma((many,)),
            dma((1,)), dma((1,)),
        ],
        compiler_params=pltpu.CompilerParams(
            collective_id=0, has_side_effects=True, vmem_limit_bytes=60 * 2**20
        ),
    )(scaled, target, stiffness)
    return out.transpose(0, 2, 1, 3)


def solution(mesh):
    in_specs = (P(None, "gz", "gy", "gx"), P("gz", "gy", "gx"))
    out_specs = P(None, "gz", "gy", "gx")
    ny, nz = mesh.shape["gy"], mesh.shape["gz"]

    def local(load_cases, density_level):
        oz, oy, ox = density_level.shape
        fits = mesh.shape["gx"] == load_cases.shape[0] == 2
        fits = fits and ox == 128 and oz % 32 == 0 and oy % 8 == 0 and min(ny, nz) >= 3
        if fits:
            return split_cases(ny, nz, load_cases, density_level)
        return body(load_cases, density_level)

    return jax.shard_map(local, mesh=mesh, in_specs=in_specs, out_specs=out_specs, check_vma=False)
```

```python
import math

import jax
import jax.numpy as jnp
from jax import lax
from jax.experimental import pallas as pl
from jax.experimental.pallas import tpu as pltpu
from jax.sharding import PartitionSpec as P

LEVELS = 8


middle_point = 0.646875
half_range = 0.503125
first_weight = 1.0 / (middle_point + half_range * math.cos(math.pi / 4))
second_weight = 1.0 / (middle_point - half_range * math.cos(math.pi / 4))


def with_halo(cells, sides, width):
    for axis, dim in sides:
        count = lax.axis_size(axis)
        ends = count - 1
        head = lax.slice_in_dim(cells, 0, width, axis=dim)
        tail = lax.slice_in_dim(cells, cells.shape[dim] - width, cells.shape[dim], axis=dim)
        cells = jnp.concatenate(
            [
                lax.ppermute(tail, axis, [(i, (i + 1) % count) for i in range(ends)]),
                cells,
                lax.ppermute(head, axis, [((i + 1) % count, i) for i in range(ends)]),
            ],
            axis=dim,
        )
    return cells


def smooth_sum(padded):
    padded = 0.5 * padded[:, :-2] + padded[:, 1:-1] + 0.5 * padded[:, 2:]
    padded = 0.5 * padded[:, :, :-2] + padded[:, :, 1:-1] + 0.5 * padded[:, :, 2:]
    return 0.5 * padded[..., :-2] + padded[..., 1:-1] + 0.5 * padded[..., 2:]


def prune(values, have, want):
    cut = have - want
    if cut == 0:
        return values
    return values[
        :, cut : values.shape[1] - cut, cut : values.shape[2] - cut, cut : values.shape[3] - cut
    ]


def inside(own, halo):
    flags = []
    for axis, size in zip(("gz", "gy", "gx"), own):
        start = lax.axis_index(axis) * size
        index = start - halo + lax.iota(jnp.int32, size + 2 * halo)
        flags.append((index >= 0) & (index < size * lax.axis_size(axis)))
    return (
        flags[0][:, None, None] & flags[1][None, :, None] & flags[2][None, None, :]
    ).astype(jnp.float32)


def step(guess, scaled, weight, mask):
    centre = prune(guess, 1, 0)
    applied = (16.0 * centre - 2.0 * smooth_sum(guess)) * (1.0 / 14.0)
    return centre + weight * (scaled - mask * applied)


def restrict(values):
    return values.reshape(
        values.shape[0], values.shape[1] // 2, 2, values.shape[2] // 2, 2, values.shape[3] // 2, 2
    ).mean(axis=(2, 4, 6))


def prolong(values):
    return jnp.repeat(jnp.repeat(jnp.repeat(values, 2, axis=1), 2, axis=2), 2, axis=3)


def framed(values, width=1):
    return jnp.pad(values, ((0, 0), (width, width), (width, width), (width, width)))


def residual(target, stiffness, guess, spacing_sq):
    centre = prune(guess, 1, 0)
    return target - stiffness * (16.0 * centre - 2.0 * smooth_sum(guess)) * (1.0 / spacing_sq)


def coarse_cycle(rhs_low, stiffness_low):
    scaled_low = rhs_low * (16.0 / (14.0 * stiffness_low))
    guess_low = step(framed(first_weight * scaled_low), scaled_low, second_weight, 1.0)
    rhs_base = restrict(residual(rhs_low, stiffness_low, framed(guess_low), 16.0))
    stiffness_base = restrict(stiffness_low)
    scaled_base = rhs_base * (64.0 / (14.0 * stiffness_base))
    guess_base = step(framed(first_weight * scaled_base), scaled_base, second_weight, 1.0)
    guess_base = step(framed(guess_base), scaled_base, first_weight, 1.0)
    guess_base = step(framed(guess_base), scaled_base, second_weight, 1.0)
    guess_low = guess_low + prolong(guess_base)
    guess_low = step(framed(guess_low), scaled_low, first_weight, 1.0)
    return step(framed(guess_low), scaled_low, second_weight, 1.0)


def joined(values):
    for axis, dim in (("gx", 3), ("gy", 2), ("gz", 1)):
        values = lax.all_gather(values, axis, axis=dim, tiled=True)
    return values


SIDES = (("gx", 3), ("gy", 2), ("gz", 1))


def body(load_cases, density_level):
    stiffness_fine = (0.05 + 0.95 * (density_level.astype(jnp.float32) / (LEVELS - 1)) ** 3)[None]
    stiffness_mid = restrict(stiffness_fine)
    stiffness_low = restrict(stiffness_mid)
    own = load_cases.shape[1:]
    own_mid = tuple(size // 2 for size in own)
    own_low = tuple(size // 4 for size in own)
    scaled_fine = with_halo(load_cases * (1.0 / (14.0 * stiffness_fine)), SIDES, 3)
    mask_fine = inside(own, 2)
    guess_fine = step(
        first_weight * scaled_fine, prune(scaled_fine, 3, 2), second_weight, mask_fine
    )
    rhs_mid = restrict(residual(load_cases, stiffness_fine, prune(guess_fine, 2, 1), 1.0))
    scaled_mid = with_halo(rhs_mid * (4.0 / (14.0 * stiffness_mid)), SIDES, 4)
    mask_mid = inside(own_mid, 3)
    guess_mid = step(first_weight * scaled_mid, prune(scaled_mid, 4, 3), second_weight, mask_mid)
    rhs_low = restrict(residual(rhs_mid, stiffness_mid, prune(guess_mid, 3, 1), 4.0))
    guess_low = framed(coarse_cycle(joined(rhs_low), joined(stiffness_low)), 2)
    guess_low = lax.dynamic_slice(
        guess_low,
        (0,) + tuple(lax.axis_index(a) * n for a, n in zip(("gz", "gy", "gx"), own_low)),
        (guess_low.shape[0],) + tuple(n + 4 for n in own_low),
    )
    guess_mid = guess_mid + prune(prolong(guess_low), 4, 3)
    guess_mid = step(guess_mid, prune(scaled_mid, 4, 2), first_weight, prune(mask_mid[None], 3, 2))
    guess_mid = step(guess_mid, prune(scaled_mid, 4, 1), second_weight, prune(mask_mid[None], 3, 1))
    guess_fine = guess_fine + prolong(guess_mid)
    guess_fine = step(
        guess_fine, prune(scaled_fine, 3, 1), first_weight, prune(mask_fine[None], 2, 1)
    )
    return step(guess_fine, prune(scaled_fine, 3, 0), second_weight, 1.0)


def parts(a):
    high = a.astype(jnp.bfloat16)
    return high, (a - high.astype(jnp.float32)).astype(jnp.bfloat16)


def product(a, b):
    return jnp.dot(a, b, preferred_element_type=jnp.float32)


def dot_right(a, matrix):
    high, low = parts(a)
    matrix = matrix.astype(jnp.bfloat16)
    return product(high, matrix) + product(low, matrix)


def dot_left(matrix, a):
    high, low = parts(a)
    matrix = matrix.astype(jnp.bfloat16)
    return product(matrix, high) + product(matrix, low)


def iota(shape, dim):
    return lax.broadcasted_iota(jnp.int32, shape, dim)


def pick(condition):
    return jnp.where(condition, 1.0, 0.0).astype(jnp.float32)


def blur(u, close_z=False):
    rows, depth, length = u.shape
    v = u[1:-1] + 0.5 * (u[:-2] + u[2:])
    down, up = pltpu.roll(v, 1, 1), pltpu.roll(v, depth - 1, 1)
    if close_z:
        z = iota((1, depth, length), 1)
        down, up = down * pick(z > 0), up * pick(z < depth - 1)
    v = v + 0.5 * (down + up)
    x = iota((1, 1, length), 2)
    down, up = pltpu.roll(v, 1, 2) * pick(x > 0), pltpu.roll(v, length - 1, 2) * pick(x < length - 1)
    return v + 0.5 * (down + up)


def move(guess, scaled, weight, mask):
    applied = (16.0 / 14.0) * guess[1:-1] - (2.0 / 14.0) * blur(guess)
    return (guess[1:-1] + weight * (scaled - applied)) * mask


def move_whole(guess, scaled, weight, mask):
    edge = jnp.zeros((1,) + guess.shape[1:], jnp.float32)
    total = blur(jnp.concatenate([edge, guess, edge], 0), True)
    return (guess + weight * (scaled - ((16.0 / 14.0) * guess - (2.0 / 14.0) * total))) * mask


def halve(values, length_out, first=0):
    rows, depth, length = values.shape
    values = values.reshape(rows // 2, 2, depth, length)
    values = values[:, 0] + values[:, 1]
    pairs = (rows // 2) * depth
    across = pick(iota((length, length_out), 0) // 2 + first == iota((length, length_out), 1)) * 0.125
    along = pick(iota((pairs // 2, pairs), 1) // 2 == iota((pairs // 2, pairs), 0))
    flat = dot_left(along, dot_right(values.reshape(pairs, length), across))
    return flat.reshape(rows // 2, depth // 2, length_out)


def double(values, depth_out, offset, length_out):
    rows, depth, length = values.shape
    across = pick(iota((length, length_out), 1) // 2 == iota((length, length_out), 0))
    along = pick(iota((depth_out, depth), 0) // 2 + offset == iota((depth_out, depth), 1))
    wide = dot_right(values.reshape(rows * depth, length), across).reshape(rows, depth, length_out)
    tall = [dot_left(along, wide[row]) for row in range(rows)]
    return jnp.stack([tall[row // 2] for row in range(2 * rows)], 0)


def domain(rows, depth, length, halo_y, halo_z, own_y, own_z, me_y, me_z, ny, nz):
    y = iota((rows, 1, length), 0) + (me_y * own_y - halo_y)
    z = iota((1, depth, length), 1) + (me_z * own_z - halo_z)
    return pick((y >= 0) & (y < own_y * ny)) * pick((z >= 0) & (z < own_z * nz))


SHIFTS = tuple((dy, dz) for dy in (-1, 0, 1) for dz in (-1, 0, 1))


def kernel(ny, nz, g_ref, s_ref, out_ref, gbuf, sbuf, mbuf, lbuf, wide, obuf, rbuf,
           send_a, recv_a, send_b, recv_b, send_c, recv_c, send_d, recv_d):
    c, my, mz = lax.axis_index("gx"), lax.axis_index("gy"), lax.axis_index("gz")
    other = 1 - c
    oy, oz, ox = s_ref.shape

    def at(k, y, z):
        return {"gx": k, "gy": y, "gz": z}

    def near(dy, dz):
        return lax.rem(my + dy + ny, ny), lax.rem(mz + dz + nz, nz)

    def group(step):
        index = lax.rem(my * nz + mz + step, ny * nz)
        return index // nz, lax.rem(index, nz)

    barrier = pltpu.get_barrier_semaphore()
    for step in range(1, ny * nz):
        pl.semaphore_signal(barrier, 1, device_id=at(c, *group(step)), device_id_type=pl.DeviceIdType.MESH)
    for shift in SHIFTS:
        pl.semaphore_signal(barrier, 1, device_id=at(other, *near(*shift)), device_id_type=pl.DeviceIdType.MESH)
    gbuf[c, 3 : 3 + oy, 8 : 8 + oz, :] = g_ref[c]
    sbuf[c] = s_ref[...]
    pl.semaphore_wait(barrier, ny * nz - 1 + 9)

    def remote(src, dst, sends, recvs, slot, device):
        copy = pltpu.make_async_remote_copy(
            src_ref=src, dst_ref=dst, send_sem=sends.at[slot], recv_sem=recvs.at[slot],
            device_id=device, device_id_type=pl.DeviceIdType.MESH,
        )
        return copy

    def exists(dy, dz):
        return (my + dy >= 0) & (my + dy < ny) & (mz + dz >= 0) & (mz + dz < nz)

    def start_all(phase):
        for copy, (dy, dz) in phase:
            pl.when(exists(dy, dz))(copy.start)

    def wait_all(phase):
        for copy, (dy, dz) in phase:
            pl.when(exists(dy, dz))(copy.wait_send)
            pl.when(exists(-dy, -dz))(copy.wait_recv)

    def cut(shift, own, reach, room):
        if shift == 0:
            return 0, room, own
        return (own - reach, room - reach, reach) if shift > 0 else (0, room + own, reach)

    phase = []
    slot = 0
    for k, who in ((0, other), (1, c)):
        for dy, dz in SHIFTS:
            if k == 1 and (dy, dz) == (0, 0):
                continue
            fy, ty, ly = cut(dy, oy, 3, 3)
            fz, tz, lz = cut(dz, oz, 8, 8)
            phase.append((remote(
                g_ref.at[who, fy : fy + ly, fz : fz + lz, :],
                gbuf.at[c, ty : ty + ly, tz : tz + lz, :],
                send_a, recv_a, slot, at(who, *near(dy, dz)),
            ), (dy, dz)))
            slot += 1
    start_all(phase)
    stiff_copy = remote(s_ref, sbuf.at[c], send_a, recv_a, slot, at(other, my, mz))
    stiff_copy.start()
    wait_all(phase)

    length = 2 * ox
    depth = oz + 16
    def mask_fine(halo):
        return domain(oy + 2 * halo, depth, length, halo, 8, oy, oz, my, mz, ny, nz)
    scaled = jnp.where(mask_fine(3) > 0.0, jnp.concatenate([gbuf[0], gbuf[1]], -1), 0.0)
    guess = move(first_weight * scaled, scaled[1:-1], second_weight, mask_fine(2))
    applied = 16.0 * guess[2:-2] - 2.0 * blur(guess[1:-1])
    stiff_copy.wait()
    stiff = jnp.concatenate([sbuf[0], sbuf[1]], -1)
    rhs_mid = halve(stiff * (14.0 * scaled[3:-3] - applied)[:, 8 : 8 + oz], ox)
    stiff_mid = halve(stiff, ox)

    hy, hz = oy // 2, oz // 2
    mbuf[4 : 4 + hy, 8 : 8 + hz, :] = rhs_mid * (4.0 / (14.0 * stiff_mid))
    phase = []
    for slot, (dy, dz) in enumerate(shift for shift in SHIFTS if shift != (0, 0)):
        fy, ty, ly = cut(dy, hy, 4, 4)
        fz, tz, lz = cut(dz, hz, 8, 8)
        phase.append((remote(
            mbuf.at[4 + fy : 4 + fy + ly, 8 + fz : 8 + fz + lz, :],
            mbuf.at[ty : ty + ly, tz : tz + lz, :],
            send_b, recv_b, slot, at(c, *near(dy, dz)),
        ), (dy, dz)))
    start_all(phase)
    packed_stiff = halve(stiff_mid, ox, ox // 2)
    wait_all(phase)

    def mask_mid(halo):
        return domain(hy + 2 * halo, hz + 16, ox, halo, 8, hy, hz, my, mz, ny, nz)
    scaled_mid = jnp.where(mask_mid(4) > 0.0, mbuf[...], 0.0)
    guess_mid = move(first_weight * scaled_mid, scaled_mid[1:-1], second_weight, mask_mid(3))
    applied = 16.0 * guess_mid[3:-3] - 2.0 * blur(guess_mid[2:-2])
    residue = rhs_mid - stiff_mid * applied[:, 8 : 8 + hz] * 0.25

    qy, qz = oy // 4, oz // 4
    lbuf[mz, my] = halve(residue, ox) + packed_stiff
    phase = []
    for step in range(1, ny * nz):
        phase.append(remote(
            lbuf.at[mz, my], lbuf.at[mz, my], send_c, recv_c, step - 1, at(c, *group(step))
        ))
    for copy in phase:
        copy.start()
    for copy in phase:
        copy.wait()
    packed = jnp.concatenate(
        [jnp.concatenate([lbuf[z, y] for y in range(ny)], 0) for z in range(nz)], 1
    )
    x = iota((1, 1, ox), 2)
    mask_low, mask_base = pick(x < ox // 2), pick(x < ox // 4)
    rhs_low = packed * mask_low
    stiff_low = pltpu.roll(packed, ox // 2, 2) * mask_low + (1.0 - mask_low)
    scaled_low = rhs_low * (16.0 / (14.0 * stiff_low))
    guess_low = move_whole(first_weight * scaled_low, scaled_low, second_weight, mask_low)
    edge = jnp.zeros((1,) + guess_low.shape[1:], jnp.float32)
    applied = 16.0 * guess_low - 2.0 * blur(jnp.concatenate([edge, guess_low, edge], 0), True)
    rhs_base = halve((rhs_low - stiff_low * applied * 0.0625) * mask_low, ox)
    stiff_base = halve(stiff_low, ox) * mask_base + (1.0 - mask_base)
    scaled_base = rhs_base * (64.0 / (14.0 * stiff_base))
    guess_base = move_whole(first_weight * scaled_base, scaled_base, second_weight, mask_base)
    guess_base = move_whole(guess_base, scaled_base, first_weight, mask_base)
    guess_base = move_whole(guess_base, scaled_base, second_weight, mask_base)
    guess_low = guess_low + double(guess_base, qz * nz, 0, ox)
    guess_low = move_whole(guess_low, scaled_low, first_weight, mask_low)
    guess_low = move_whole(guess_low, scaled_low, second_weight, mask_low)

    wide[...] = jnp.zeros(wide.shape, jnp.float32)
    wide[2 : 2 + qy * ny, 8 : 8 + qz * nz, :] = guess_low
    around = wide[pl.ds(my * qy, qy + 4), pl.ds(pl.multiple_of(mz * qz, 8), qz + 16), :]
    guess_mid = guess_mid + double(around, hz + 16, 4, ox)[1:-1]
    guess_mid = move(guess_mid, scaled_mid[2:-2], first_weight, mask_mid(2))
    guess_mid = move(guess_mid, scaled_mid[3:-3], second_weight, mask_mid(1))
    guess = guess + double(guess_mid, depth, 4, length)
    guess = move(guess, scaled[2:-2], first_weight, mask_fine(1))
    guess = move(guess, scaled[3:-3], second_weight, 1.0)[:, 8 : 8 + oz]

    obuf[0] = guess[:, :, :ox]
    obuf[1] = guess[:, :, ox:]
    copy = remote(obuf.at[other], rbuf, send_d, recv_d, 0, at(other, my, mz))
    copy.start()
    out_ref[c] = obuf[c]
    copy.wait()
    out_ref[other] = rbuf[...]


def split_cases(ny, nz, load_cases, density_level):
    stiffness = (0.05 + 0.95 * (density_level.astype(jnp.float32) / (LEVELS - 1)) ** 3)
    stiffness = stiffness.transpose(1, 0, 2)
    scaled = load_cases.transpose(0, 2, 1, 3) * (1.0 / (14.0 * stiffness))
    oy, oz, ox = stiffness.shape
    f32 = jnp.float32
    spec = pl.BlockSpec(memory_space=pltpu.VMEM)
    dma = pltpu.SemaphoreType.DMA
    many = ny * nz - 1
    out = pl.pallas_call(
        lambda *refs: kernel(ny, nz, *refs),
        out_shape=jax.ShapeDtypeStruct(scaled.shape, f32),
        in_specs=[spec] * 2,
        out_specs=spec,
        scratch_shapes=[
            pltpu.VMEM((2, oy + 6, oz + 16, ox), f32),
            pltpu.VMEM((2, oy, oz, ox), f32),
            pltpu.VMEM((oy // 2 + 8, oz // 2 + 16, ox), f32),
            pltpu.VMEM((nz, ny, oy // 4, oz // 4, ox), f32),
            pltpu.VMEM((oy // 4 * ny + 4, oz // 4 * nz + 16, ox), f32),
            pltpu.VMEM((2, oy, oz, ox), f32),
            pltpu.VMEM((oy, oz, ox), f32),
            dma((18,)), dma((18,)), dma((8,)), dma((8,)), dma((many,)), dma((many,)),
            dma((1,)), dma((1,)),
        ],
        compiler_params=pltpu.CompilerParams(
            collective_id=0, has_side_effects=True, vmem_limit_bytes=60 * 2**20
        ),
    )(scaled, stiffness)
    return out.transpose(0, 2, 1, 3)


def solution(mesh):
    in_specs = (P(None, "gz", "gy", "gx"), P("gz", "gy", "gx"))
    out_specs = P(None, "gz", "gy", "gx")
    ny, nz = mesh.shape["gy"], mesh.shape["gz"]

    def local(load_cases, density_level):
        oz, oy, ox = density_level.shape
        fits = mesh.shape["gx"] == load_cases.shape[0] == 2
        fits = fits and ox == 128 and oz % 32 == 0 and oy % 8 == 0 and min(ny, nz) >= 3
        if fits:
            return split_cases(ny, nz, load_cases, density_level)
        return body(load_cases, density_level)

    return jax.shard_map(local, mesh=mesh, in_specs=in_specs, out_specs=out_specs, check_vma=False)
```

```python
import math

import jax
import jax.numpy as jnp
from jax import lax
from jax.experimental import pallas as pl
from jax.experimental.pallas import tpu as pltpu
from jax.sharding import PartitionSpec as P

LEVELS = 8


middle_point = 0.646875
half_range = 0.503125
first_weight = 1.0 / (middle_point + half_range * math.cos(math.pi / 4))
second_weight = 1.0 / (middle_point - half_range * math.cos(math.pi / 4))


def with_halo(cells, sides, width):
    for axis, dim in sides:
        count = lax.axis_size(axis)
        ends = count - 1
        head = lax.slice_in_dim(cells, 0, width, axis=dim)
        tail = lax.slice_in_dim(cells, cells.shape[dim] - width, cells.shape[dim], axis=dim)
        cells = jnp.concatenate(
            [
                lax.ppermute(tail, axis, [(i, (i + 1) % count) for i in range(ends)]),
                cells,
                lax.ppermute(head, axis, [((i + 1) % count, i) for i in range(ends)]),
            ],
            axis=dim,
        )
    return cells


def smooth_sum(padded):
    padded = 0.5 * padded[:, :-2] + padded[:, 1:-1] + 0.5 * padded[:, 2:]
    padded = 0.5 * padded[:, :, :-2] + padded[:, :, 1:-1] + 0.5 * padded[:, :, 2:]
    return 0.5 * padded[..., :-2] + padded[..., 1:-1] + 0.5 * padded[..., 2:]


def prune(values, have, want):
    cut = have - want
    if cut == 0:
        return values
    return values[
        :, cut : values.shape[1] - cut, cut : values.shape[2] - cut, cut : values.shape[3] - cut
    ]


def inside(own, halo):
    flags = []
    for axis, size in zip(("gz", "gy", "gx"), own):
        start = lax.axis_index(axis) * size
        index = start - halo + lax.iota(jnp.int32, size + 2 * halo)
        flags.append((index >= 0) & (index < size * lax.axis_size(axis)))
    return (
        flags[0][:, None, None] & flags[1][None, :, None] & flags[2][None, None, :]
    ).astype(jnp.float32)


def step(guess, scaled, weight, mask):
    centre = prune(guess, 1, 0)
    applied = (16.0 * centre - 2.0 * smooth_sum(guess)) * (1.0 / 14.0)
    return centre + weight * (scaled - mask * applied)


def restrict(values):
    return values.reshape(
        values.shape[0], values.shape[1] // 2, 2, values.shape[2] // 2, 2, values.shape[3] // 2, 2
    ).mean(axis=(2, 4, 6))


def prolong(values):
    return jnp.repeat(jnp.repeat(jnp.repeat(values, 2, axis=1), 2, axis=2), 2, axis=3)


def framed(values, width=1):
    return jnp.pad(values, ((0, 0), (width, width), (width, width), (width, width)))


def residual(target, stiffness, guess, spacing_sq):
    centre = prune(guess, 1, 0)
    return target - stiffness * (16.0 * centre - 2.0 * smooth_sum(guess)) * (1.0 / spacing_sq)


def coarse_cycle(rhs_low, stiffness_low):
    scaled_low = rhs_low * (16.0 / (14.0 * stiffness_low))
    guess_low = step(framed(first_weight * scaled_low), scaled_low, second_weight, 1.0)
    rhs_base = restrict(residual(rhs_low, stiffness_low, framed(guess_low), 16.0))
    stiffness_base = restrict(stiffness_low)
    scaled_base = rhs_base * (64.0 / (14.0 * stiffness_base))
    guess_base = step(framed(first_weight * scaled_base), scaled_base, second_weight, 1.0)
    guess_base = step(framed(guess_base), scaled_base, first_weight, 1.0)
    guess_base = step(framed(guess_base), scaled_base, second_weight, 1.0)
    guess_low = guess_low + prolong(guess_base)
    guess_low = step(framed(guess_low), scaled_low, first_weight, 1.0)
    return step(framed(guess_low), scaled_low, second_weight, 1.0)


def joined(values):
    for axis, dim in (("gx", 3), ("gy", 2), ("gz", 1)):
        values = lax.all_gather(values, axis, axis=dim, tiled=True)
    return values


SIDES = (("gx", 3), ("gy", 2), ("gz", 1))


def body(load_cases, density_level):
    stiffness_fine = (0.05 + 0.95 * (density_level.astype(jnp.float32) / (LEVELS - 1)) ** 3)[None]
    stiffness_mid = restrict(stiffness_fine)
    stiffness_low = restrict(stiffness_mid)
    own = load_cases.shape[1:]
    own_mid = tuple(size // 2 for size in own)
    own_low = tuple(size // 4 for size in own)
    scaled_fine = with_halo(load_cases * (1.0 / (14.0 * stiffness_fine)), SIDES, 3)
    mask_fine = inside(own, 2)
    guess_fine = step(
        first_weight * scaled_fine, prune(scaled_fine, 3, 2), second_weight, mask_fine
    )
    rhs_mid = restrict(residual(load_cases, stiffness_fine, prune(guess_fine, 2, 1), 1.0))
    scaled_mid = with_halo(rhs_mid * (4.0 / (14.0 * stiffness_mid)), SIDES, 4)
    mask_mid = inside(own_mid, 3)
    guess_mid = step(first_weight * scaled_mid, prune(scaled_mid, 4, 3), second_weight, mask_mid)
    rhs_low = restrict(residual(rhs_mid, stiffness_mid, prune(guess_mid, 3, 1), 4.0))
    guess_low = framed(coarse_cycle(joined(rhs_low), joined(stiffness_low)), 2)
    guess_low = lax.dynamic_slice(
        guess_low,
        (0,) + tuple(lax.axis_index(a) * n for a, n in zip(("gz", "gy", "gx"), own_low)),
        (guess_low.shape[0],) + tuple(n + 4 for n in own_low),
    )
    guess_mid = guess_mid + prune(prolong(guess_low), 4, 3)
    guess_mid = step(guess_mid, prune(scaled_mid, 4, 2), first_weight, prune(mask_mid[None], 3, 2))
    guess_mid = step(guess_mid, prune(scaled_mid, 4, 1), second_weight, prune(mask_mid[None], 3, 1))
    guess_fine = guess_fine + prolong(guess_mid)
    guess_fine = step(
        guess_fine, prune(scaled_fine, 3, 1), first_weight, prune(mask_fine[None], 2, 1)
    )
    return step(guess_fine, prune(scaled_fine, 3, 0), second_weight, 1.0)


def parts(a):
    high = a.astype(jnp.bfloat16)
    return high, (a - high.astype(jnp.float32)).astype(jnp.bfloat16)


def product(a, b):
    return jnp.dot(a, b, preferred_element_type=jnp.float32)


def dot_right(a, matrix):
    high, low = parts(a)
    matrix = matrix.astype(jnp.bfloat16)
    return product(high, matrix) + product(low, matrix)


def dot_left(matrix, a):
    high, low = parts(a)
    matrix = matrix.astype(jnp.bfloat16)
    return product(matrix, high) + product(matrix, low)


def iota(shape, dim):
    return lax.broadcasted_iota(jnp.int32, shape, dim)


def pick(condition):
    return jnp.where(condition, 1.0, 0.0).astype(jnp.float32)


def blur(u, close_z=False):
    rows, depth, length = u.shape
    v = u[1:-1] + 0.5 * (u[:-2] + u[2:])
    down, up = pltpu.roll(v, 1, 1), pltpu.roll(v, depth - 1, 1)
    if close_z:
        z = iota((1, depth, length), 1)
        down, up = down * pick(z > 0), up * pick(z < depth - 1)
    v = v + 0.5 * (down + up)
    x = iota((1, 1, length), 2)
    down, up = pltpu.roll(v, 1, 2) * pick(x > 0), pltpu.roll(v, length - 1, 2) * pick(x < length - 1)
    return v + 0.5 * (down + up)


def move(guess, scaled, weight, mask):
    applied = (16.0 / 14.0) * guess[1:-1] - (2.0 / 14.0) * blur(guess)
    return (guess[1:-1] + weight * (scaled - applied)) * mask


def move_whole(guess, scaled, weight, mask):
    edge = jnp.zeros((1,) + guess.shape[1:], jnp.float32)
    total = blur(jnp.concatenate([edge, guess, edge], 0), True)
    return (guess + weight * (scaled - ((16.0 / 14.0) * guess - (2.0 / 14.0) * total))) * mask


def halve(values, length_out, first=0):
    rows, depth, length = values.shape
    values = values.reshape(rows // 2, 2, depth, length)
    values = values[:, 0] + values[:, 1]
    pairs = (rows // 2) * depth
    across = pick(iota((length, length_out), 0) // 2 + first == iota((length, length_out), 1)) * 0.125
    along = pick(iota((pairs // 2, pairs), 1) // 2 == iota((pairs // 2, pairs), 0))
    flat = dot_left(along, dot_right(values.reshape(pairs, length), across))
    return flat.reshape(rows // 2, depth // 2, length_out)


def double(values, depth_out, offset, length_out):
    rows, depth, length = values.shape
    across = pick(iota((length, length_out), 1) // 2 == iota((length, length_out), 0))
    along = pick(iota((depth_out, depth), 0) // 2 + offset == iota((depth_out, depth), 1))
    wide = dot_right(values.reshape(rows * depth, length), across).reshape(rows, depth, length_out)
    tall = [dot_left(along, wide[row]) for row in range(rows)]
    return jnp.stack([tall[row // 2] for row in range(2 * rows)], 0)


def domain(rows, depth, length, halo_y, halo_z, own_y, own_z, me_y, me_z, ny, nz):
    y = iota((rows, 1, length), 0) + (me_y * own_y - halo_y)
    z = iota((1, depth, length), 1) + (me_z * own_z - halo_z)
    return pick((y >= 0) & (y < own_y * ny)) * pick((z >= 0) & (z < own_z * nz))


SHIFTS = tuple((dy, dz) for dy in (-1, 0, 1) for dz in (-1, 0, 1))


def kernel(ny, nz, g_ref, s_ref, out_ref, gbuf, sbuf, mbuf, lbuf, wide, obuf, rbuf,
           send_a, recv_a, send_b, recv_b, send_c, recv_c, send_d, recv_d):
    c, my, mz = lax.axis_index("gx"), lax.axis_index("gy"), lax.axis_index("gz")
    other = 1 - c
    oy, oz, ox = s_ref.shape

    def at(k, y, z):
        return {"gx": k, "gy": y, "gz": z}

    def near(dy, dz):
        return lax.rem(my + dy + ny, ny), lax.rem(mz + dz + nz, nz)

    def group(step):
        index = lax.rem(my * nz + mz + step, ny * nz)
        return index // nz, lax.rem(index, nz)

    barrier = pltpu.get_barrier_semaphore()
    for step in range(1, ny * nz):
        pl.semaphore_signal(barrier, 1, device_id=at(c, *group(step)), device_id_type=pl.DeviceIdType.MESH)
    for shift in SHIFTS:
        pl.semaphore_signal(barrier, 1, device_id=at(other, *near(*shift)), device_id_type=pl.DeviceIdType.MESH)
    gbuf[c, 3 : 3 + oy, 8 : 8 + oz, :] = g_ref[c]
    sbuf[c] = s_ref[...]
    pl.semaphore_wait(barrier, ny * nz - 1 + 9)

    def remote(src, dst, sends, recvs, slot, device):
        copy = pltpu.make_async_remote_copy(
            src_ref=src, dst_ref=dst, send_sem=sends.at[slot], recv_sem=recvs.at[slot],
            device_id=device, device_id_type=pl.DeviceIdType.MESH,
        )
        return copy

    def exists(dy, dz):
        return (my + dy >= 0) & (my + dy < ny) & (mz + dz >= 0) & (mz + dz < nz)

    def start_all(phase):
        for copy, (dy, dz) in phase:
            pl.when(exists(dy, dz))(copy.start)

    def wait_all(phase):
        for copy, (dy, dz) in phase:
            pl.when(exists(dy, dz))(copy.wait_send)
            pl.when(exists(-dy, -dz))(copy.wait_recv)

    def cut(shift, own, reach, room):
        if shift == 0:
            return 0, room, own
        return (own - reach, room - reach, reach) if shift > 0 else (0, room + own, reach)

    phase = []
    slot = 0
    for k, who in ((0, other), (1, c)):
        for dy, dz in SHIFTS:
            if k == 1 and (dy, dz) == (0, 0):
                continue
            fy, ty, ly = cut(dy, oy, 3, 3)
            fz, tz, lz = cut(dz, oz, 8, 8)
            phase.append((remote(
                g_ref.at[who, fy : fy + ly, fz : fz + lz, :],
                gbuf.at[c, ty : ty + ly, tz : tz + lz, :],
                send_a, recv_a, slot, at(who, *near(dy, dz)),
            ), (dy, dz)))
            slot += 1
    start_all(phase)
    stiff_copy = remote(s_ref, sbuf.at[c], send_a, recv_a, slot, at(other, my, mz))
    stiff_copy.start()
    wait_all(phase)

    length = 2 * ox
    depth = oz + 16
    def mask_fine(halo):
        return domain(oy + 2 * halo, depth, length, halo, 8, oy, oz, my, mz, ny, nz)
    scaled = jnp.where(mask_fine(3) > 0.0, jnp.concatenate([gbuf[0], gbuf[1]], -1), 0.0)
    guess = move(first_weight * scaled, scaled[1:-1], second_weight, mask_fine(2))
    applied = 16.0 * guess[2:-2] - 2.0 * blur(guess[1:-1])
    stiff_copy.wait()
    stiff = jnp.concatenate([sbuf[0], sbuf[1]], -1)
    rhs_mid = halve(stiff * (14.0 * scaled[3:-3] - applied)[:, 8 : 8 + oz], ox)
    stiff_mid = halve(stiff, ox)

    hy, hz = oy // 2, oz // 2
    mbuf[4 : 4 + hy, 8 : 8 + hz, :] = rhs_mid * (4.0 / (14.0 * stiff_mid))
    phase = []
    for slot, (dy, dz) in enumerate(shift for shift in SHIFTS if shift != (0, 0)):
        fy, ty, ly = cut(dy, hy, 4, 4)
        fz, tz, lz = cut(dz, hz, 8, 8)
        phase.append((remote(
            mbuf.at[4 + fy : 4 + fy + ly, 8 + fz : 8 + fz + lz, :],
            mbuf.at[ty : ty + ly, tz : tz + lz, :],
            send_b, recv_b, slot, at(c, *near(dy, dz)),
        ), (dy, dz)))
    start_all(phase)
    packed_stiff = halve(stiff_mid, ox, ox // 2)
    wait_all(phase)

    def mask_mid(halo):
        return domain(hy + 2 * halo, hz + 16, ox, halo, 8, hy, hz, my, mz, ny, nz)
    scaled_mid = jnp.where(mask_mid(4) > 0.0, mbuf[...], 0.0)
    guess_mid = move(first_weight * scaled_mid, scaled_mid[1:-1], second_weight, mask_mid(3))
    applied = 16.0 * guess_mid[3:-3] - 2.0 * blur(guess_mid[2:-2])
    residue = rhs_mid - stiff_mid * applied[:, 8 : 8 + hz] * 0.25

    qy, qz = oy // 4, oz // 4
    lbuf[mz, my] = halve(residue, ox) + packed_stiff
    phase = []
    for step in range(1, ny * nz):
        phase.append(remote(
            lbuf.at[mz, my], lbuf.at[mz, my], send_c, recv_c, step - 1, at(c, *group(step))
        ))
    for copy in phase:
        copy.start()
    for copy in phase:
        copy.wait()
    packed = jnp.concatenate(
        [jnp.concatenate([lbuf[z, y] for y in range(ny)], 0) for z in range(nz)], 1
    )
    x = iota((1, 1, ox), 2)
    mask_low, mask_base = pick(x < ox // 2), pick(x < ox // 4)
    rhs_low = packed * mask_low
    stiff_low = pltpu.roll(packed, ox // 2, 2) * mask_low + (1.0 - mask_low)
    scaled_low = rhs_low * (16.0 / (14.0 * stiff_low))
    guess_low = move_whole(first_weight * scaled_low, scaled_low, second_weight, mask_low)
    edge = jnp.zeros((1,) + guess_low.shape[1:], jnp.float32)
    applied = 16.0 * guess_low - 2.0 * blur(jnp.concatenate([edge, guess_low, edge], 0), True)
    rhs_base = halve((rhs_low - stiff_low * applied * 0.0625) * mask_low, ox)
    stiff_base = halve(stiff_low, ox) * mask_base + (1.0 - mask_base)
    scaled_base = rhs_base * (64.0 / (14.0 * stiff_base))
    guess_base = move_whole(first_weight * scaled_base, scaled_base, second_weight, mask_base)
    guess_base = move_whole(guess_base, scaled_base, first_weight, mask_base)
    guess_base = move_whole(guess_base, scaled_base, second_weight, mask_base)
    guess_low = guess_low + double(guess_base, qz * nz, 0, ox)
    guess_low = move_whole(guess_low, scaled_low, first_weight, mask_low)
    guess_low = move_whole(guess_low, scaled_low, second_weight, mask_low)

    wide[...] = jnp.zeros(wide.shape, jnp.float32)
    wide[2 : 2 + qy * ny, 8 : 8 + qz * nz, :] = guess_low
    around = wide[pl.ds(my * qy, qy + 4), pl.ds(pl.multiple_of(mz * qz, 8), qz + 16), :]
    guess_mid = guess_mid + double(around, hz + 16, 4, ox)[1:-1]
    guess_mid = move(guess_mid, scaled_mid[2:-2], first_weight, mask_mid(2))
    guess_mid = move(guess_mid, scaled_mid[3:-3], second_weight, mask_mid(1))
    guess = guess + double(guess_mid, depth, 4, length)
    guess = move(guess, scaled[2:-2], first_weight, mask_fine(1))
    phase = []
    rows = oy // 4
    for slot in range(4):
        first, last = slot * rows, slot * rows + rows
        piece = move(guess[first : last + 2], scaled[3 + first : 3 + last], second_weight, 1.0)
        piece = piece[:, 8 : 8 + oz]
        obuf[0, first:last] = piece[:, :, :ox]
        obuf[1, first:last] = piece[:, :, ox:]
        copy = remote(
            obuf.at[other, first:last], rbuf.at[first:last], send_d, recv_d, slot, at(other, my, mz)
        )
        copy.start()
        phase.append(copy)
    out_ref[c] = obuf[c]
    for copy in phase:
        copy.wait()
    out_ref[other] = rbuf[...]


def split_cases(ny, nz, load_cases, density_level):
    stiffness = (0.05 + 0.95 * (density_level.astype(jnp.float32) / (LEVELS - 1)) ** 3)
    stiffness = stiffness.transpose(1, 0, 2)
    scaled = load_cases.transpose(0, 2, 1, 3) * (1.0 / (14.0 * stiffness))
    oy, oz, ox = stiffness.shape
    f32 = jnp.float32
    spec = pl.BlockSpec(memory_space=pltpu.VMEM)
    dma = pltpu.SemaphoreType.DMA
    many = ny * nz - 1
    out = pl.pallas_call(
        lambda *refs: kernel(ny, nz, *refs),
        out_shape=jax.ShapeDtypeStruct(scaled.shape, f32),
        in_specs=[spec] * 2,
        out_specs=spec,
        scratch_shapes=[
            pltpu.VMEM((2, oy + 6, oz + 16, ox), f32),
            pltpu.VMEM((2, oy, oz, ox), f32),
            pltpu.VMEM((oy // 2 + 8, oz // 2 + 16, ox), f32),
            pltpu.VMEM((nz, ny, oy // 4, oz // 4, ox), f32),
            pltpu.VMEM((oy // 4 * ny + 4, oz // 4 * nz + 16, ox), f32),
            pltpu.VMEM((2, oy, oz, ox), f32),
            pltpu.VMEM((oy, oz, ox), f32),
            dma((18,)), dma((18,)), dma((8,)), dma((8,)), dma((many,)), dma((many,)),
            dma((4,)), dma((4,)),
        ],
        compiler_params=pltpu.CompilerParams(
            collective_id=0, has_side_effects=True, vmem_limit_bytes=60 * 2**20
        ),
    )(scaled, stiffness)
    return out.transpose(0, 2, 1, 3)


def solution(mesh):
    in_specs = (P(None, "gz", "gy", "gx"), P("gz", "gy", "gx"))
    out_specs = P(None, "gz", "gy", "gx")
    ny, nz = mesh.shape["gy"], mesh.shape["gz"]

    def local(load_cases, density_level):
        oz, oy, ox = density_level.shape
        fits = mesh.shape["gx"] == load_cases.shape[0] == 2
        fits = fits and ox == 128 and oz % 32 == 0 and oy % 8 == 0 and min(ny, nz) >= 3
        if fits:
            return split_cases(ny, nz, load_cases, density_level)
        return body(load_cases, density_level)

    return jax.shard_map(local, mesh=mesh, in_specs=in_specs, out_specs=out_specs, check_vma=False)
```
